128 devices in a mesh: row: 8 (over y, x_lo), col: 16 (over z, x_hi, core).
Axes of the slice: x: 4 (x_hi: 2, x_lo: 2; x = x_hi * 2 + x_lo), y: 4, z: 4, core: 2. Of those that a mesh axis runs over, the one named last changes fastest.
Arguments:
- gradient: float32 [6144, 12288], P(('row', 'col')), may hold values from -200 to 200
Outputs:
- preconditioned: float32 [6144, 12288], P(('row', 'col'))
The draws below stay inside these ranges and needn't reach their ends.
All inputs are finite; a program needn't handle non-finite values.
Results may differ from the reference program's by a relative error of at most 0.00023.
Values sent between devices are 32-bit elements; how exact they have to be, the bound alone decides.
No kernel may reach another device: no remote copies, remote signals or barrier semaphores. Data moves between devices by JAX's collectives and lax.ppermute only.
A program may use at most 64 MiB of HBM per device.

```python
import math
import jax
import jax.numpy as jnp
from jax import lax

D = 12288
R = 6144
BLOCK = 768
ITERS = 2


def draw_gradient(key, part):
    keys = jax.random.split(jax.random.fold_in(key, 17), 3)
    row_scale = jnp.exp(jax.random.uniform(keys[0], (R, 1), jnp.float32, 0.0, math.log(10.0)))
    col_scale = jnp.exp(jax.random.uniform(keys[1], (1, D), jnp.float32, 0.0, math.log(3.0)))
    values = jax.random.normal(keys[2], (R, D), jnp.float32) * row_scale * col_scale
    return jnp.clip(values, -200.0, 200.0).astype(jnp.float32)


def setup_inputs(seed: int = 0) -> dict:
    arg_keys = jax.random.split(jax.random.key(seed), 2)
    gradient = draw_gradient(jax.random.fold_in(arg_keys[1], 71), 0)
    return dict(gradient=gradient)


def product(first, second):
    return jnp.matmul(first, second, precision=lax.Precision.HIGHEST)

def inverse_root(gram_matrix):
    matrix_order = gram_matrix.shape[-1]
    identity = jnp.eye(matrix_order, dtype=gram_matrix.dtype)
    norm_scale = jnp.sqrt(lax.optimization_barrier(jnp.sum(gram_matrix * gram_matrix, axis=(-2, -1), keepdims=True))) + 1e-06
    iterate = gram_matrix / norm_scale
    root_now = identity
    for iteration in range(ITERS):
        factor = (5.0 * identity - iterate) * 0.25
        root_now = factor if iteration == 0 else product(root_now, factor)
        if iteration + 1 < ITERS:
            square = product(factor, factor)
            iterate = product(product(square, square), iterate)
    return root_now * norm_scale ** (-0.25)

def reference(gradient):
    block_count = D // BLOCK
    row_count = R // BLOCK
    blocks = gradient.reshape(row_count, BLOCK, block_count, BLOCK)
    left_gram = jnp.einsum('aibj,akbj->aik', blocks, blocks, precision=lax.Precision.HIGHEST) / D
    right_gram = jnp.einsum('aibj,aibk->bjk', blocks, blocks, precision=lax.Precision.HIGHEST) / D
    left_roots = inverse_root(left_gram)
    right_roots = inverse_root(right_gram)
    mixed_rows = jnp.einsum('aik,akbj->aibj', left_roots, blocks, precision=lax.Precision.HIGHEST)
    result = jnp.einsum('aibj,bjl->aibl', mixed_rows, right_roots, precision=lax.Precision.HIGHEST)
    return result.reshape(R, D)
```

```python
import jax
import jax.numpy as jnp
from jax import lax
from jax.experimental import pallas as pl
from jax.experimental.pallas import tpu as pltpu
from jax.sharding import Mesh
from jax.sharding import PartitionSpec as P

D = 12288
N = 768
T = 256
B = 128
EDGE = N // B
PAIRS = [(i, j) for j in range(EDGE) for i in range(j + 1)]
PACKED = len(PAIRS) * B
RPART = PACKED // 4
LHALF = PACKED // 2
LPART = LHALF // 4
COL = ("z", "xh", "core")
ALL = ("y", "xl", "z", "xh", "core")
C0, C1, C2, C3, C4, C5, C6 = (
    c / 4096.0 for c in (6400.0, -4405.0, 3125.0, -1250.0, 250.0, -25.0, 1.0)
)
f32, bf16 = jnp.float32, jnp.bfloat16


def halves(x):
    high = x.astype(bf16)
    return high, (x - high.astype(f32)).astype(bf16)


def product3(ah, al, bh, bl, dims):
    def dot(p, q):
        return lax.dot_general(p, q, (dims, ((), ())), preferred_element_type=f32)

    return dot(ah, bh) + dot(ah, bl) + dot(al, bh)


def pack_panel(panel, j, packed):
    for bj in range(j * T // B, (j + 1) * T // B):
        for bi in range(bj + 1):
            k = PAIRS.index((bi, bj))
            packed[k * B : (k + 1) * B, :] = panel[
                bi * B : (bi + 1) * B, bj * B - j * T : (bj + 1) * B - j * T
            ]


def piece(packed, index, rows):
    return packed[pl.ds(pl.multiple_of(index * rows, 8), rows), :]


def gram_right(where, tile, own, one, two, three, high, low, packed):
    high[...], low[...] = halves(tile[...])
    for j in range(N // T):
        rows, cols = slice(0, (j + 1) * T), slice(j * T, (j + 1) * T)
        panel = product3(
            high[:, rows], low[:, rows], high[:, cols], low[:, cols], ((0,), (0,))
        )
        pack_panel(panel * (1.0 / D), j, packed)
    y = where[0]
    for k, out in enumerate((own, one, two, three)):
        out[...] = piece(packed, lax.rem(y + k, 4), RPART)


def gram_left(where, tile, keep, send, high, low, packed):
    high[...], low[...] = halves(tile[...])
    for j in range(N // T):
        rows, cols = slice(0, (j + 1) * T), slice(j * T, (j + 1) * T)
        panel = product3(high[rows], low[rows], high[cols], low[cols], ((1,), (1,)))
        pack_panel(panel * (1.0 / D), j, packed)
    core = where[2]
    keep[...] = piece(packed, core, LHALF)
    send[...] = piece(packed, 1 - core, LHALF)


def cut_left(where, keep, received, own, one, two, three, total):
    total[...] = keep[...] + received[...]
    z = where[1]
    for k, out in enumerate((own, one, two, three)):
        out[...] = piece(total, lax.rem(z + k, 4), LPART)


def symmetric_product(a, b, out):
    for j in range(N // T):
        rows, cols = slice(0, (j + 1) * T), slice(j * T, (j + 1) * T)
        panel = product3(a[0][rows], a[1][rows], b[0][:, cols], b[1][:, cols], ((1,), (0,)))
        out[rows, cols] = panel
        for i in range(j):
            out[cols, i * T : (i + 1) * T] = panel[i * T : (i + 1) * T].T


def root_of(packed, m, m2, m3, mh, ml, ah, al, bh, bl):
    total = jnp.zeros((B, B), f32)
    for k, (i, j) in enumerate(PAIRS):
        block = packed[k * B : (k + 1) * B, :]
        total = total + block * block * (1.0 if i == j else 2.0)
    norm = jnp.sqrt(jnp.sum(jnp.sum(total, axis=0, keepdims=True), axis=1, keepdims=True)) + 1e-06
    inverse = 1.0 / norm
    scale = lax.rsqrt(jnp.sqrt(norm))
    for k, (i, j) in enumerate(PAIRS):
        block = packed[k * B : (k + 1) * B, :] * inverse
        m[i * B : (i + 1) * B, j * B : (j + 1) * B] = block
        if i != j:
            m[j * B : (j + 1) * B, i * B : (i + 1) * B] = block.T
    eye = (
        lax.broadcasted_iota(jnp.int32, (N, N), 0) == lax.broadcasted_iota(jnp.int32, (N, N), 1)
    ).astype(f32)
    mh[...], ml[...] = halves(m[...])
    symmetric_product((mh, ml), (mh, ml), m2)
    ah[...], al[...] = halves(m2[...])
    symmetric_product((ah, al), (mh, ml), m3)
    ah[...], al[...] = halves(m3[...])
    bh[...], bl[...] = halves(C6 * m3[...] + C5 * m2[...] + C4 * m[...] + C3 * eye)
    symmetric_product((ah, al), (bh, bl), m3)
    root = (m3[...] + C2 * m2[...] + C1 * m[...] + C0 * eye) * scale
    ah[...], al[...] = halves(root)


def apply_left(where, *refs):
    parts, tile, out, packed = refs[:8], refs[8], refs[9], refs[10]
    work = refs[11:]
    z, core = where[1], where[2]
    for k in range(8):
        half = core if k < 4 else 1 - core
        start = pl.multiple_of(half * LHALF + lax.rem(z + 4 - k % 4, 4) * LPART, 8)
        packed[pl.ds(start, LPART), :] = parts[k][...]
    root_of(packed, *work)
    ah, al, bh, bl = work[5:]
    bh[...], bl[...] = halves(tile[...])
    for j in range(N // T):
        cols = slice(j * T, (j + 1) * T)
        out[:, cols] = product3(ah[...], al[...], bh[:, cols], bl[:, cols], ((1,), (0,)))


def apply_right(where, *refs):
    parts, mixed, out, packed = refs[:4], refs[4], refs[5], refs[6]
    work = refs[7:]
    y = where[0]
    for k in range(4):
        start = pl.multiple_of(lax.rem(y + 4 - k, 4) * RPART, 8)
        packed[pl.ds(start, RPART), :] = parts[k][...]
    root_of(packed, *work)
    ah, al, bh, bl = work[5:]
    bh[...], bl[...] = halves(mixed[...])
    for j in range(N // T):
        cols = slice(j * T, (j + 1) * T)
        out[:, cols] = product3(bh[...], bl[...], ah[:, cols], al[:, cols], ((1,), (0,)))


HALF = pltpu.VMEM((N, N), bf16)
WHOLE = pltpu.VMEM((N, N), f32)
PACK = pltpu.VMEM((PACKED, B), f32)
ROOT = [PACK, WHOLE, WHOLE, WHOLE] + [HALF] * 6


def call(body, name, outs, scratch, args, products):
    vmem = pl.BlockSpec(memory_space=pltpu.VMEM)
    return pl.pallas_call(
        body,
        out_shape=[jax.ShapeDtypeStruct(s, f32) for s in outs],
        in_specs=[pl.BlockSpec(memory_space=pltpu.SMEM)] + [vmem] * (len(args) - 1),
        out_specs=[vmem] * len(outs),
        scratch_shapes=scratch,
        name=name,
        cost_estimate=pl.CostEstimate(
            flops=int(products * 2 * N**3), bytes_accessed=2 * N * N * 4, transcendentals=0
        ),
        compiler_params=pltpu.CompilerParams(vmem_limit_bytes=40 << 20),
    )(*args)


def shift(x, axis, k):
    return lax.ppermute(x, axis, [(i, (i + k) % 4) for i in range(4)])


def swap(x, axis):
    return lax.ppermute(x, axis, [(0, 1), (1, 0)])


def local(gradient):
    where = jnp.stack([lax.axis_index("y"), lax.axis_index("z"), lax.axis_index("core")])
    tile = lax.all_to_all(gradient, COL, split_axis=1, concat_axis=0, tiled=True)

    right = call(gram_right, "gram_right", [(RPART, B)] * 4, [HALF, HALF, PACK], (where, tile), 2)
    arrived = [shift(right[k], "y", k) for k in (1, 2, 3)]
    keep, send = call(gram_left, "gram_left", [(LHALF, B)] * 2, [HALF, HALF, PACK], (where, tile), 2)
    half = pltpu.VMEM((LHALF, B), f32)
    left = call(
        cut_left, "cut_left", [(LPART, B)] * 4, [half], (where, keep, swap(send, "core")), 0
    )
    left_sum = left[0] + sum(shift(left[k], "z", k) for k in (1, 2, 3))
    left_sum = left_sum + swap(left_sum, "xh")
    mine = [left_sum] + [shift(left_sum, "z", k) for k in (1, 2, 3)]
    theirs = [swap(part, "core") for part in mine]

    right_sum = right[0] + arrived[0] + arrived[1] + arrived[2]
    right_sum = right_sum + swap(right_sum, "xl")
    right_parts = [right_sum] + [shift(right_sum, "y", k) for k in (1, 2, 3)]

    (mixed,) = call(apply_left, "apply_left", [(N, N)], ROOT, (where, *mine, *theirs, tile), 8)
    (result,) = call(apply_right, "apply_right", [(N, N)], ROOT, (where, *right_parts, mixed), 8)
    return lax.all_to_all(result, COL, split_axis=0, concat_axis=1, tiled=True)


def solution(mesh):
    split = Mesh(mesh.devices.reshape(4, 2, 4, 2, 2), ALL)
    placed = P(ALL, None)
    return jax.shard_map(local, mesh=split, in_specs=(placed,), out_specs=placed, check_vma=False)
```

```python
import jax
import jax.numpy as jnp
from jax import lax
from jax.experimental import pallas as pl
from jax.experimental.pallas import tpu as pltpu
from jax.sharding import Mesh
from jax.sharding import PartitionSpec as P

D = 12288
N = 768
T = 256
B = 128
EDGE = N // B
PAIRS = [(i, j) for j in range(EDGE) for i in range(j + 1)]
PACKED = len(PAIRS) * B
RPART = PACKED // 4
LHALF = PACKED // 2
LPART = LHALF // 4
PEERS = [(0, 0), (0, 1), (2, 0), (1, 1), (3, 0), (2, 1), (1, 0), (3, 1)]
EARLY = 5
ROWS = N // 16
ALL = ("y", "xl", "z", "xh", "core")
C0, C1, C2, C3, C4, C5, C6 = (
    c / 4096.0 for c in (6400.0, -4405.0, 3125.0, -1250.0, 250.0, -25.0, 1.0)
)
f32, bf16 = jnp.float32, jnp.bfloat16


def halves(x):
    high = x.astype(bf16)
    return high, (x - high.astype(f32)).astype(bf16)


def product3(ah, al, bh, bl, dims):
    def dot(p, q):
        return lax.dot_general(p, q, (dims, ((), ())), preferred_element_type=f32)

    return dot(ah, bh) + dot(ah, bl) + dot(al, bh)


def pack_panel(panel, j, packed):
    for bj in range(j * T // B, (j + 1) * T // B):
        for bi in range(bj + 1):
            k = PAIRS.index((bi, bj))
            packed[k * B : (k + 1) * B, :] = panel[
                bi * B : (bi + 1) * B, bj * B - j * T : (bj + 1) * B - j * T
            ]


def piece(packed, index, rows):
    return packed[pl.ds(pl.multiple_of(index * rows, 8), rows), :]


def peer_chip(where, k, sign):
    dz, dx = PEERS[k]
    return lax.rem(where[1] + 4 + sign * dz, 4) * 2 + lax.rem(where[3] + dx, 2)


def cut_in(where, gradient, *refs):
    outs, sems = refs[:-1], refs[-1]
    copies = []
    for k, out in enumerate(outs):
        for j in range(2):
            start = pl.multiple_of((peer_chip(where, k, 1) * 2 + j) * N, B)
            copies.append(
                pltpu.make_async_copy(gradient.at[:, pl.ds(start, N)], out.at[j], sems.at[k, j])
            )
    for copy in copies:
        copy.start()
    for copy in copies:
        copy.wait()


def pick(where, *refs):
    arrived, out = refs[:-1], refs[-1]
    for k, ref in enumerate(arrived):
        out[k] = ref[1 - where[2]]


def put_out(where, *refs):
    arrived, early, late, out, sems = refs[:8], refs[8], refs[9], refs[10], refs[11]
    copies = []
    for k in range(8):
        block = peer_chip(where, k, -1) * 2
        other = early.at[k] if k < EARLY else late.at[k - EARLY]
        for j, source in enumerate((arrived[k].at[where[2]], other)):
            column = block + (where[2] if j == 0 else 1 - where[2])
            target = out.at[:, pl.ds(pl.multiple_of(column * N, B), N)]
            copies.append(pltpu.make_async_copy(source, target, sems.at[k, j]))
    for copy in copies:
        copy.start()
    for copy in copies:
        copy.wait()


def gram_right(where, *refs):
    arrived, early, late = refs[:8], refs[8], refs[9]
    own, one, two, three, tile, high, low, packed = refs[10:]
    core = where[2]
    for k in range(8):
        first = peer_chip(where, k, -1) * 2
        other = early[k] if k < EARLY else late[k - EARLY]
        for index, rows in ((first + core, arrived[k][core]), (first + 1 - core, other)):
            tile[pl.ds(pl.multiple_of(index * ROWS, 8), ROWS), :] = rows
    high[...], low[...] = halves(tile[...])
    for j in range(N // T):
        rows, cols = slice(0, (j + 1) * T), slice(j * T, (j + 1) * T)
        panel = product3(
            high[:, rows], low[:, rows], high[:, cols], low[:, cols], ((0,), (0,))
        )
        pack_panel(panel * (1.0 / D), j, packed)
    y = where[0]
    for k, out in enumerate((own, one, two, three)):
        out[...] = piece(packed, lax.rem(y + k, 4), RPART)


def gram_left(where, tile, keep, send, high, low, packed):
    high[...], low[...] = halves(tile[...])
    for j in range(N // T):
        rows, cols = slice(0, (j + 1) * T), slice(j * T, (j + 1) * T)
        panel = product3(high[rows], low[rows], high[cols], low[cols], ((1,), (1,)))
        pack_panel(panel * (1.0 / D), j, packed)
    core = where[2]
    keep[...] = piece(packed, core, LHALF)
    send[...] = piece(packed, 1 - core, LHALF)


def cut_left(where, keep, received, own, one, two, three, total):
    total[...] = keep[...] + received[...]
    z = where[1]
    for k, out in enumerate((own, one, two, three)):
        out[...] = piece(total, lax.rem(z + k, 4), LPART)


def symmetric_product(a, b, out):
    for j in range(N // T):
        rows, cols = slice(0, (j + 1) * T), slice(j * T, (j + 1) * T)
        panel = product3(a[0][rows], a[1][rows], b[0][:, cols], b[1][:, cols], ((1,), (0,)))
        out[rows, cols] = panel
        for i in range(j):
            out[cols, i * T : (i + 1) * T] = panel[i * T : (i + 1) * T].T


def root_of(packed, m, m2, m3, mh, ml, ah, al, bh, bl):
    total = jnp.zeros((B, B), f32)
    for k, (i, j) in enumerate(PAIRS):
        block = packed[k * B : (k + 1) * B, :]
        total = total + block * block * (1.0 if i == j else 2.0)
    norm = jnp.sqrt(jnp.sum(jnp.sum(total, axis=0, keepdims=True), axis=1, keepdims=True)) + 1e-06
    inverse = 1.0 / norm
    scale = lax.rsqrt(jnp.sqrt(norm))
    for k, (i, j) in enumerate(PAIRS):
        block = packed[k * B : (k + 1) * B, :] * inverse
        m[i * B : (i + 1) * B, j * B : (j + 1) * B] = block
        if i != j:
            m[j * B : (j + 1) * B, i * B : (i + 1) * B] = block.T
    eye = (
        lax.broadcasted_iota(jnp.int32, (N, N), 0) == lax.broadcasted_iota(jnp.int32, (N, N), 1)
    ).astype(f32)
    mh[...], ml[...] = halves(m[...])
    symmetric_product((mh, ml), (mh, ml), m2)
    ah[...], al[...] = halves(m2[...])
    symmetric_product((ah, al), (mh, ml), m3)
    ah[...], al[...] = halves(m3[...])
    bh[...], bl[...] = halves(C6 * m3[...] + C5 * m2[...] + C4 * m[...] + C3 * eye)
    symmetric_product((ah, al), (bh, bl), m3)
    root = (m3[...] + C2 * m2[...] + C1 * m[...] + C0 * eye) * scale
    ah[...], al[...] = halves(root)


def apply_left(where, *refs):
    parts, tile, out, packed = refs[:8], refs[8], refs[9], refs[10]
    work = refs[11:]
    z, core = where[1], where[2]
    for k in range(8):
        half = core if k < 4 else 1 - core
        start = pl.multiple_of(half * LHALF + lax.rem(z + 4 - k % 4, 4) * LPART, 8)
        packed[pl.ds(start, LPART), :] = parts[k][...]
    root_of(packed, *work)
    ah, al, bh, bl = work[5:]
    bh[...], bl[...] = halves(tile[...])
    for j in range(N // T):
        cols = slice(j * T, (j + 1) * T)
        out[:, cols] = product3(ah[...], al[...], bh[:, cols], bl[:, cols], ((1,), (0,)))


def apply_right(where, *refs):
    parts, mixed, outs, packed = refs[:4], refs[4], refs[5:13], refs[13]
    work = refs[14:]
    y = where[0]
    for k in range(4):
        start = pl.multiple_of(lax.rem(y + 4 - k, 4) * RPART, 8)
        packed[pl.ds(start, RPART), :] = parts[k][...]
    root_of(packed, *work)
    ah, al, bh, bl = work[5:]
    result = work[0]
    bh[...], bl[...] = halves(mixed[...])
    for j in range(N // T):
        cols = slice(j * T, (j + 1) * T)
        result[:, cols] = product3(bh[...], bl[...], ah[:, cols], al[:, cols], ((1,), (0,)))
    for k, out in enumerate(outs):
        for j in range(2):
            index = peer_chip(where, k, 1) * 2 + j
            out[j] = result[pl.ds(pl.multiple_of(index * ROWS, 8), ROWS), :]


HALF = pltpu.VMEM((N, N), bf16)
WHOLE = pltpu.VMEM((N, N), f32)
PACK = pltpu.VMEM((PACKED, B), f32)
ROOT = [PACK, WHOLE, WHOLE, WHOLE] + [HALF] * 6


VMEM = pl.BlockSpec(memory_space=pltpu.VMEM)
HBM = pl.BlockSpec(memory_space=pltpu.HBM)
COPIES = pltpu.SemaphoreType.DMA((8, 2))


def call(body, name, outs, scratch, args, products, source=VMEM, target=VMEM):
    return pl.pallas_call(
        body,
        out_shape=[jax.ShapeDtypeStruct(s, f32) for s in outs],
        in_specs=[pl.BlockSpec(memory_space=pltpu.SMEM)] + [source] * (len(args) - 1),
        out_specs=[target] * len(outs),
        scratch_shapes=scratch,
        name=name,
        cost_estimate=pl.CostEstimate(
            flops=int(products * 2 * N**3), bytes_accessed=2 * N * N * 4, transcendentals=0
        ),
        compiler_params=pltpu.CompilerParams(vmem_limit_bytes=32 << 20),
    )(*args)


def shift(x, axis, k):
    return lax.ppermute(x, axis, [(i, (i + k) % 4) for i in range(4)])


def swap(x, axis):
    return lax.ppermute(x, axis, [(0, 1), (1, 0)])


def exchange(where, sent):
    arrived = [sent[0]]
    for k in range(7, 0, -1):
        dz, dx = PEERS[k]
        pairs = [
            (z * 2 + x, (z + dz) % 4 * 2 + (x + dx) % 2) for z in range(4) for x in range(2)
        ]
        arrived.insert(1, lax.ppermute(sent[k], ("z", "xh"), pairs))
    others = []
    for name, part in (("pick_early", arrived[:EARLY]), ("pick_late", arrived[EARLY:])):
        (other,) = call(pick, name, [(len(part), ROWS, N)], [], (where, *part), 0)
        others.append(swap(other, "core"))
    return (*arrived, *others)


def local(gradient):
    where = jnp.stack([lax.axis_index(axis) for axis in ("y", "z", "core", "xh")])
    sent = call(cut_in, "cut_in", [(2, ROWS, N)] * 8, [COPIES], (where, gradient), 0, source=HBM)
    arrived = exchange(where, sent)

    *right, tile = call(
        gram_right,
        "gram_right",
        [(RPART, B)] * 4 + [(N, N)],
        [HALF, HALF, PACK],
        (where, *arrived),
        2,
    )
    right_arrived = [shift(right[k], "y", k) for k in (1, 2, 3)]
    keep, send = call(gram_left, "gram_left", [(LHALF, B)] * 2, [HALF, HALF, PACK], (where, tile), 2)
    half = pltpu.VMEM((LHALF, B), f32)
    left = call(
        cut_left, "cut_left", [(LPART, B)] * 4, [half], (where, keep, swap(send, "core")), 0
    )
    left_sum = left[0] + sum(shift(left[k], "z", k) for k in (1, 2, 3))
    left_sum = left_sum + swap(left_sum, "xh")
    mine = [left_sum] + [shift(left_sum, "z", k) for k in (1, 2, 3)]
    theirs = [swap(part, "core") for part in mine]

    right_sum = right[0] + right_arrived[0] + right_arrived[1] + right_arrived[2]
    right_sum = right_sum + swap(right_sum, "xl")
    right_parts = [right_sum] + [shift(right_sum, "y", k) for k in (1, 2, 3)]

    (mixed,) = call(apply_left, "apply_left", [(N, N)], ROOT, (where, *mine, *theirs, tile), 8)
    sent = call(
        apply_right, "apply_right", [(2, ROWS, N)] * 8, ROOT, (where, *right_parts, mixed), 8
    )
    arrived = exchange(where, sent)
    (out,) = call(put_out, "put_out", [(ROWS, 16 * N)], [COPIES], (where, *arrived), 0, target=HBM)
    return out


def solution(mesh):
    split = Mesh(mesh.devices.reshape(4, 2, 4, 2, 2), ALL)
    placed = P(ALL, None)
    return jax.shard_map(local, mesh=split, in_specs=(placed,), out_specs=placed, check_vma=False)
```

```python
import functools

import jax
import jax.numpy as jnp
from jax import lax
from jax.experimental import pallas as pl
from jax.experimental.pallas import tpu as pltpu
from jax.sharding import Mesh
from jax.sharding import PartitionSpec as P

D = 12288
N = 768
T = 256
B = 128
EDGE = N // B
PAIRS = [(i, j) for j in range(EDGE) for i in range(j + 1)]
PACKED = len(PAIRS) * B
RPART = PACKED // 4
LHALF = PACKED // 2
LPART = LHALF // 4
PEERS = [(0, 0), (0, 1), (2, 0), (1, 1), (3, 0), (2, 1), (1, 0), (3, 1)]
EARLY = 5
ROWS = N // 16
ALL = ("y", "xl", "z", "xh", "core")
C0, C1, C2, C3, C4, C5, C6 = (
    c / 4096.0 for c in (6400.0, -4405.0, 3125.0, -1250.0, 250.0, -25.0, 1.0)
)
f32, bf16 = jnp.float32, jnp.bfloat16


def halves(x):
    high = x.astype(bf16)
    return high, (x - high.astype(f32)).astype(bf16)


def product3(ah, al, bh, bl, dims):
    def dot(p, q):
        return lax.dot_general(p, q, (dims, ((), ())), preferred_element_type=f32)

    return dot(ah, bh) + dot(ah, bl) + dot(al, bh)


def pack_panel(panel, j, packed):
    for bj in range(j * T // B, (j + 1) * T // B):
        for bi in range(bj + 1):
            k = PAIRS.index((bi, bj))
            packed[k * B : (k + 1) * B, :] = panel[
                bi * B : (bi + 1) * B, bj * B - j * T : (bj + 1) * B - j * T
            ]


def piece(packed, index, rows):
    return packed[pl.ds(pl.multiple_of(index * rows, 8), rows), :]


def peer_chip(where, k, sign):
    dz, dx = PEERS[k]
    return lax.rem(where[1] + 4 + sign * dz, 4) * 2 + lax.rem(where[3] + dx, 2)


def cut_in(where, gradient, *refs):
    outs, sems = refs[:-1], refs[-1]
    copies = []
    for k, out in enumerate(outs):
        for j in range(2):
            start = pl.multiple_of((peer_chip(where, k, 1) * 2 + j) * N, B)
            copies.append(
                pltpu.make_async_copy(gradient.at[:, pl.ds(start, N)], out.at[j], sems.at[k, j])
            )
    for copy in copies:
        copy.start()
    for copy in copies:
        copy.wait()


def pick(where, *refs):
    arrived, out = refs[:-1], refs[-1]
    for k, ref in enumerate(arrived):
        out[k] = ref[1 - where[2]]


def put_out(blocks, *refs):
    where, out, sems = refs[0], refs[-2], refs[-1]
    copies = []
    for n, (operand, entry, peer, own) in enumerate(blocks):
        core = where[2] if own else 1 - where[2]
        column = peer_chip(where, peer, -1) * 2 + core
        copies.append(
            pltpu.make_async_copy(
                refs[operand].at[where[2] if entry is None else entry],
                out.at[:, pl.ds(pl.multiple_of(column * N, B), N)],
                sems.at[n // 2, n % 2],
            )
        )
    for copy in copies:
        copy.start()
    for copy in copies:
        copy.wait()


def own_blocks(first, peers):
    return [(first + n, None, k, True) for n, k in enumerate(peers)]


def other_blocks(operand, peers):
    return [(operand, n, k, False) for n, k in enumerate(peers)]


def gram_right(where, *refs):
    arrived, early, late = refs[:8], refs[8], refs[9]
    own, one, two, three, tile, high, low, packed = refs[10:]
    core = where[2]
    for k in range(8):
        first = peer_chip(where, k, -1) * 2
        other = early[k] if k < EARLY else late[k - EARLY]
        for index, rows in ((first + core, arrived[k][core]), (first + 1 - core, other)):
            tile[pl.ds(pl.multiple_of(index * ROWS, 8), ROWS), :] = rows
    high[...], low[...] = halves(tile[...])
    for j in range(N // T):
        rows, cols = slice(0, (j + 1) * T), slice(j * T, (j + 1) * T)
        panel = product3(
            high[:, rows], low[:, rows], high[:, cols], low[:, cols], ((0,), (0,))
        )
        pack_panel(panel * (1.0 / D), j, packed)
    y = where[0]
    for k, out in enumerate((own, one, two, three)):
        out[...] = piece(packed, lax.rem(y + k, 4), RPART)


def gram_left(where, tile, keep, send, high, low, packed):
    high[...], low[...] = halves(tile[...])
    for j in range(N // T):
        rows, cols = slice(0, (j + 1) * T), slice(j * T, (j + 1) * T)
        panel = product3(high[rows], low[rows], high[cols], low[cols], ((1,), (1,)))
        pack_panel(panel * (1.0 / D), j, packed)
    core = where[2]
    keep[...] = piece(packed, core, LHALF)
    send[...] = piece(packed, 1 - core, LHALF)


def cut_left(where, keep, received, own, one, two, three, total):
    total[...] = keep[...] + received[...]
    z = where[1]
    for k, out in enumerate((own, one, two, three)):
        out[...] = piece(total, lax.rem(z + k, 4), LPART)


def symmetric_product(a, b, out):
    for j in range(N // T):
        rows, cols = slice(0, (j + 1) * T), slice(j * T, (j + 1) * T)
        panel = product3(a[0][rows], a[1][rows], b[0][:, cols], b[1][:, cols], ((1,), (0,)))
        out[rows, cols] = panel
        for i in range(j):
            out[cols, i * T : (i + 1) * T] = panel[i * T : (i + 1) * T].T


def root_of(packed, m, m2, m3, mh, ml, ah, al, bh, bl):
    total = jnp.zeros((B, B), f32)
    for k, (i, j) in enumerate(PAIRS):
        block = packed[k * B : (k + 1) * B, :]
        total = total + block * block * (1.0 if i == j else 2.0)
    norm = jnp.sqrt(jnp.sum(jnp.sum(total, axis=0, keepdims=True), axis=1, keepdims=True)) + 1e-06
    inverse = 1.0 / norm
    scale = lax.rsqrt(jnp.sqrt(norm))
    for k, (i, j) in enumerate(PAIRS):
        block = packed[k * B : (k + 1) * B, :] * inverse
        m[i * B : (i + 1) * B, j * B : (j + 1) * B] = block
        if i != j:
            m[j * B : (j + 1) * B, i * B : (i + 1) * B] = block.T
    eye = (
        lax.broadcasted_iota(jnp.int32, (N, N), 0) == lax.broadcasted_iota(jnp.int32, (N, N), 1)
    ).astype(f32)
    mh[...], ml[...] = halves(m[...])
    symmetric_product((mh, ml), (mh, ml), m2)
    ah[...], al[...] = halves(m2[...])
    symmetric_product((ah, al), (mh, ml), m3)
    ah[...], al[...] = halves(m3[...])
    bh[...], bl[...] = halves(C6 * m3[...] + C5 * m2[...] + C4 * m[...] + C3 * eye)
    symmetric_product((ah, al), (bh, bl), m3)
    root = (m3[...] + C2 * m2[...] + C1 * m[...] + C0 * eye) * scale
    ah[...], al[...] = halves(root)


def apply_left(where, *refs):
    parts, tile, out, packed = refs[:8], refs[8], refs[9], refs[10]
    work = refs[11:]
    z, core = where[1], where[2]
    for k in range(8):
        half = core if k < 4 else 1 - core
        start = pl.multiple_of(half * LHALF + lax.rem(z + 4 - k % 4, 4) * LPART, 8)
        packed[pl.ds(start, LPART), :] = parts[k][...]
    root_of(packed, *work)
    ah, al, bh, bl = work[5:]
    bh[...], bl[...] = halves(tile[...])
    for j in range(N // T):
        cols = slice(j * T, (j + 1) * T)
        out[:, cols] = product3(ah[...], al[...], bh[:, cols], bl[:, cols], ((1,), (0,)))


def apply_right(where, *refs):
    parts, mixed, outs, packed = refs[:4], refs[4], refs[5:13], refs[13]
    work = refs[14:]
    y = where[0]
    for k in range(4):
        start = pl.multiple_of(lax.rem(y + 4 - k, 4) * RPART, 8)
        packed[pl.ds(start, RPART), :] = parts[k][...]
    root_of(packed, *work)
    ah, al, bh, bl = work[5:]
    result = work[0]
    bh[...], bl[...] = halves(mixed[...])
    for j in range(N // T):
        cols = slice(j * T, (j + 1) * T)
        result[:, cols] = product3(bh[...], bl[...], ah[:, cols], al[:, cols], ((1,), (0,)))
    for k, out in enumerate(outs):
        for j in range(2):
            index = peer_chip(where, k, 1) * 2 + j
            out[j] = result[pl.ds(pl.multiple_of(index * ROWS, 8), ROWS), :]


HALF = pltpu.VMEM((N, N), bf16)
WHOLE = pltpu.VMEM((N, N), f32)
PACK = pltpu.VMEM((PACKED, B), f32)
ROOT = [PACK, WHOLE, WHOLE, WHOLE] + [HALF] * 6


VMEM = pl.BlockSpec(memory_space=pltpu.VMEM)
HBM = pl.BlockSpec(memory_space=pltpu.HBM)
COPIES = pltpu.SemaphoreType.DMA((8, 2))


def call(body, outs, scratch, args, products, source=VMEM, target=VMEM, out=None):
    specs = [source] * (len(args) - 1) + [HBM] * (out is not None)
    args = args if out is None else (*args, out)
    return pl.pallas_call(
        body,
        out_shape=[jax.ShapeDtypeStruct(s, f32) for s in outs],
        in_specs=[pl.BlockSpec(memory_space=pltpu.SMEM)] + specs,
        input_output_aliases={} if out is None else {len(args) - 1: 0},
        out_specs=[target] * len(outs),
        scratch_shapes=scratch,
        cost_estimate=pl.CostEstimate(
            flops=int(products * 2 * N**3), bytes_accessed=2 * N * N * 4, transcendentals=0
        ),
        compiler_params=pltpu.CompilerParams(vmem_limit_bytes=32 << 20),
    )(*args)


def shift(x, axis, k):
    return lax.ppermute(x, axis, [(i, (i + k) % 4) for i in range(4)])


def swap(x, axis):
    return lax.ppermute(x, axis, [(0, 1), (1, 0)])


def exchange(where, sent):
    arrived = [sent[0]]
    for k in range(7, 0, -1):
        dz, dx = PEERS[k]
        pairs = [
            (z * 2 + x, (z + dz) % 4 * 2 + (x + dx) % 2) for z in range(4) for x in range(2)
        ]
        arrived.insert(1, lax.ppermute(sent[k], ("z", "xh"), pairs))
    others = []
    for part in (arrived[:EARLY], arrived[EARLY:]):
        (other,) = call(pick, [(len(part), ROWS, N)], [], (where, *part), 0)
        others.append(swap(other, "core"))
    return (*arrived, *others)


def local(gradient):
    where = jnp.stack([lax.axis_index(axis) for axis in ("y", "z", "core", "xh")])
    in_hbm = pltpu.with_memory_space_constraint(gradient, pltpu.HBM)
    sent = call(cut_in, [(2, ROWS, N)] * 8, [COPIES], (where, in_hbm), 0, HBM)
    arrived = exchange(where, sent)

    *right, tile = call(
        gram_right, [(RPART, B)] * 4 + [(N, N)], [HALF, HALF, PACK], (where, *arrived), 2
    )
    right_arrived = [shift(right[k], "y", k) for k in (1, 2, 3)]
    keep, send = call(gram_left, [(LHALF, B)] * 2, [HALF, HALF, PACK], (where, tile), 2)
    half = pltpu.VMEM((LHALF, B), f32)
    received = swap(send, "core")
    left = call(cut_left, [(LPART, B)] * 4, [half], (where, keep, received), 0)
    left_sum = left[0] + sum(shift(left[k], "z", k) for k in (1, 2, 3))
    left_sum = left_sum + swap(left_sum, "xh")
    mine = [left_sum] + [shift(left_sum, "z", k) for k in (1, 2, 3)]
    theirs = [swap(part, "core") for part in mine]

    right_sum = right[0] + right_arrived[0] + right_arrived[1] + right_arrived[2]
    right_sum = right_sum + swap(right_sum, "xl")
    right_parts = [right_sum] + [shift(right_sum, "y", k) for k in (1, 2, 3)]

    (mixed,) = call(apply_left, [(N, N)], ROOT, (where, *mine, *theirs, tile), 8)
    sent = call(apply_right, [(2, ROWS, N)] * 8, ROOT, (where, *right_parts, mixed), 8)
    *arrived, early, late = exchange(where, sent)

    def put(operands, blocks, out):
        body = functools.partial(put_out, blocks)
        args = (where, *operands)
        return call(body, [(ROWS, 16 * N)], [COPIES], args, 0, target=HBM, out=out)[0]

    firsts, lasts = range(EARLY), range(EARLY, 8)
    out = put(arrived[:EARLY], own_blocks(1, firsts), None)
    blocks = own_blocks(1, lasts) + other_blocks(1 + len(lasts), firsts)
    out = put((*arrived[EARLY:], early), blocks, out)
    return put((late,), other_blocks(1, lasts), out)


def solution(mesh):
    split = Mesh(mesh.devices.reshape(4, 2, 4, 2, 2), ALL)
    placed = P(ALL, None)

    return jax.shard_map(local, mesh=split, in_specs=(placed,), out_specs=placed, check_vma=False)
```
